768 devices in a mesh: replica: 32 (over y, x), owner: 6 (over z_lo, core), tensor: 4 (over z_hi).
Axes of the slice: x: 4, y: 8, z: 12 (z_hi: 4, z_lo: 3; z = z_hi * 3 + z_lo), core: 2. Of those that a mesh axis runs over, the one named last changes fastest.
Arguments:
- grad_partial: bfloat16 [192, 24, 512, 512], P(('replica', 'owner'), 'tensor'), may hold values from -1 to 1
- owner_table: int32 [4, 6], P('tensor'), may hold values from 0 to 5, each once within a row
- left_factor: float32 [6, 4, 512, 512], P('owner', 'tensor'), may hold values from -1 to 4, as said below
- right_factor: float32 [6, 4, 512, 512], P('owner', 'tensor'), may hold values from -1 to 4, as said below
- left_precond: bfloat16 [6, 4, 512, 512], P('owner', 'tensor'), may hold values from -2 to 3, as said below
- right_precond: bfloat16 [6, 4, 512, 512], P('owner', 'tensor'), may hold values from -2 to 3, as said below
Outputs:
- direction: bfloat16 [24, 512, 512], P('tensor')
- new_left: float32 [6, 4, 512, 512], P('owner', 'tensor')
- new_right: float32 [6, 4, 512, 512], P('owner', 'tensor')
The draws below stay inside these ranges and needn't reach their ends.
Inputs may be any that keep to these rules, and one draw needn't show every extreme that they name: `owner_table`: each row of the table is a permutation: every owner holds exactly one block of each tensor shard. `left_factor`: Symmetric. `right_factor`: Symmetric. `left_precond`: Symmetric. `right_precond`: Symmetric.
All inputs are finite; a program needn't handle non-finite values.
Results may differ from the reference program's by a relative error of at most 0.015.
Values may be sent and summed in bfloat16 or wider, within the bound.
No kernel may reach another device: no remote copies, remote signals or barrier semaphores. Data moves between devices by JAX's collectives and lax.ppermute only.
A program may use at most 32 MiB of HBM per device.

```python
import math
import jax
import jax.numpy as jnp
from jax import lax

B = 512
KB = 6
NBLK = 24
NDATA = 192
N_OWNER = 6
N_TENSOR = 4


def draw_grad_partial(key, part):
    keys = jax.random.split(jax.random.fold_in(key, 5), 6)
    low = math.log(0.3)
    high = math.log(3.0)
    rows = jnp.exp(jax.random.uniform(keys[0], (NBLK, B, 1), jnp.float32, low, high))
    cols = jnp.exp(jax.random.uniform(keys[1], (NBLK, 1, B), jnp.float32, low, high))
    gains = jnp.exp(jax.random.uniform(keys[5], (NDATA, NBLK, 1, 1), jnp.float32, low, high))

    def one_device(index):
        local_key = jax.random.fold_in(keys[2], index)
        noise = jax.random.normal(local_key, (NBLK, B, B), jnp.float32)
        gain = lax.dynamic_index_in_dim(gains, index, 0, keepdims=False)
        values = noise * rows * cols * gain * (0.25 / math.sqrt(B))
        return jnp.clip(values, -1.0, 1.0).astype(jnp.bfloat16)
    return lax.map(one_device, jnp.arange(NDATA, dtype=jnp.int32))


def factor_helper(key):
    basis = jax.random.normal(key, (N_OWNER, N_TENSOR, B, B), jnp.float32) / math.sqrt(B)
    square = jnp.einsum('otij,otkj->otik', basis, basis, precision=lax.Precision.HIGHEST)
    return jnp.clip(square + 0.5 * jnp.eye(B, dtype=jnp.float32), -1.0, 4.0)


def precond_helper(key):
    noise = jax.random.normal(key, (N_OWNER, N_TENSOR, B, B), jnp.float32) / math.sqrt(B)
    symmetric = (noise + jnp.swapaxes(noise, 2, 3)) / math.sqrt(2.0)
    return jnp.clip(1.2 * jnp.eye(B, dtype=jnp.float32) + 0.4 * symmetric, -2.0, 3.0)


def draw_left_factor(key, part):
    return factor_helper(jax.random.fold_in(key, 11))


def draw_right_factor(key, part):
    return factor_helper(jax.random.fold_in(key, 12))


def draw_left_precond(key, part):
    return precond_helper(jax.random.fold_in(key, 21)).astype(jnp.bfloat16)


def draw_right_precond(key, part):
    return precond_helper(jax.random.fold_in(key, 22)).astype(jnp.bfloat16)


def setup_inputs(seed: int = 0) -> dict:
    arg_keys = jax.random.split(jax.random.key(seed), 7)
    grad_partial = draw_grad_partial(jax.random.fold_in(arg_keys[6], 71), 0)
    owner_table = jax.vmap(lambda own: jax.random.permutation(own, N_OWNER))(jax.random.split(arg_keys[1], N_TENSOR)).reshape((N_TENSOR, KB)).astype(jnp.int32)
    left_factor = draw_left_factor(jax.random.fold_in(arg_keys[6], 71), 0)
    right_factor = draw_right_factor(jax.random.fold_in(arg_keys[6], 71), 0)
    left_precond = draw_left_precond(jax.random.fold_in(arg_keys[6], 71), 0)
    right_precond = draw_right_precond(jax.random.fold_in(arg_keys[6], 71), 0)
    return dict(grad_partial=grad_partial, owner_table=owner_table, left_factor=left_factor, right_factor=right_factor, left_precond=left_precond, right_precond=right_precond)


decay = 0.9
epsilon = 1e-06

def reference(grad_partial, owner_table, left_factor, right_factor, left_precond, right_precond):
    highest = lax.Precision.HIGHEST

    def add_one(index, total):
        return total + lax.dynamic_index_in_dim(grad_partial, index, 0, keepdims=False).astype(jnp.float32)
    total = lax.fori_loop(0, NDATA, add_one, jnp.zeros((NBLK, B, B), jnp.float32))
    summed = total.astype(jnp.bfloat16)
    blocks = summed.reshape(N_TENSOR, KB, B, B).astype(jnp.float32)
    owners = jnp.arange(N_OWNER, dtype=jnp.int32)
    selector = (owner_table[:, :, None] == owners[None, None, :]).astype(jnp.float32)
    owned = jnp.einsum('tko,tkij->otij', selector, blocks, precision=highest)
    outer_rows = jnp.einsum('otij,otkj->otik', owned, owned, precision=highest)
    outer_cols = jnp.einsum('otji,otjk->otik', owned, owned, precision=highest)
    new_left = decay * left_factor + (1.0 - decay) * outer_rows
    new_right = decay * right_factor + (1.0 - decay) * outer_cols
    half = jnp.einsum('otij,otjk->otik', left_precond.astype(jnp.float32), owned, precision=highest).astype(jnp.bfloat16)
    full = jnp.einsum('otij,otjk->otik', half.astype(jnp.float32), right_precond.astype(jnp.float32), precision=highest)
    scaled = (full * lax.rsqrt(lax.optimization_barrier(jnp.mean(full * full, axis=(2, 3), keepdims=True)) + epsilon)).astype(jnp.bfloat16)
    tensors = jnp.arange(N_TENSOR, dtype=jnp.int32)[:, None]
    direction = scaled[owner_table, tensors]
    return (direction.reshape(NBLK, B, B), new_left, new_right)
```

```python
import jax
import jax.numpy as jnp
from jax import lax
from jax.experimental import pallas as pl
from jax.experimental.pallas import tpu as pltpu
from jax.sharding import Mesh, PartitionSpec as P

decay = 0.9
epsilon = 1e-06

NY, NX, NZ, NC, NT = 8, 4, 3, 2, 4
B = 512
ROWS = B // (NX * NY)
SWAP = [(0, 1), (1, 0)]


def assemble_kernel(pick_ref, same_ref, other_ref, out_ref, sem):
    count = out_ref.shape[0]

    def copies(k):
        o = pick_ref[k]
        z = lax.rem(o, NZ)
        return (
            o < NZ,
            pltpu.make_async_copy(same_ref.at[z], out_ref.at[k], sem.at[k]),
            pltpu.make_async_copy(other_ref.at[z], out_ref.at[k], sem.at[k]),
        )

    for k in range(count):
        near, a, b = copies(k)

        @pl.when(near)
        def _():
            a.start()

        @pl.when(jnp.logical_not(near))
        def _():
            b.start()

    for k in range(count):
        _, a, _ = copies(k)
        a.wait()


def assemble(pick, same, other):
    count = pick.shape[0]
    return pl.pallas_call(
        assemble_kernel,
        out_shape=jax.ShapeDtypeStruct((count, B, B), same.dtype),
        in_specs=[
            pl.BlockSpec(memory_space=pltpu.SMEM),
            pl.BlockSpec(memory_space=pltpu.VMEM),
            pl.BlockSpec(memory_space=pltpu.VMEM),
        ],
        out_specs=pl.BlockSpec(memory_space=pl.ANY),
        scratch_shapes=[pltpu.SemaphoreType.DMA((count,))],
        name="assemble",
    )(pick, same, other)


def local(grad_partial, owner_table, left_factor, right_factor, left_precond, right_precond):
    table_row = owner_table[0]
    core = lax.axis_index("core")
    count = table_row.shape[0]
    positions = jnp.arange(count, dtype=jnp.int32)
    slot = positions % NZ
    wanted = 2 * slot + jnp.where(positions < NZ, core, 1 - core)
    matches = table_row[None, :] == wanted[:, None]
    source = jnp.sum(jnp.where(matches, positions[None, :], 0), axis=1)
    pick = table_row // 2 + jnp.where(table_row % 2 == core, 0, NZ)

    grad = grad_partial[0]
    keep = grad.at[source[:NZ]].get(mode="promise_in_bounds")
    give = grad.at[source[NZ:]].get(mode="promise_in_bounds")
    got = lax.ppermute(give, "core", SWAP)
    pair = (keep.astype(jnp.float32) + got.astype(jnp.float32)).astype(jnp.bfloat16)
    pieces = pair.reshape(NZ, NX, NY, ROWS, B).transpose(1, 2, 0, 3, 4)
    over_x = lax.all_to_all(pieces.reshape(NX, NY * NZ * ROWS, B), "x", 0, 0)
    part = jnp.sum(over_x.astype(jnp.float32), axis=0).astype(jnp.bfloat16)
    over_yz = lax.all_to_all(part.reshape(NY * NZ, ROWS, B), ("y", "zl"), 0, 0)
    mine = jnp.sum(over_yz.astype(jnp.float32), axis=0).astype(jnp.bfloat16)

    strip = lax.all_gather(mine, "y", axis=0, tiled=True)
    owned = lax.all_gather(strip, "x", axis=0, tiled=True)

    half_product = jnp.dot(left_precond[0, 0], owned, preferred_element_type=jnp.float32).astype(
        jnp.bfloat16
    )
    full_product = jnp.dot(half_product, right_precond[0, 0], preferred_element_type=jnp.float32)
    scaled = (full_product * lax.rsqrt(jnp.mean(full_product * full_product) + epsilon)).astype(
        jnp.bfloat16
    )
    same = lax.all_to_all(jnp.broadcast_to(scaled[None], (NZ, B, B)), "zl", 0, 0)
    other = lax.ppermute(same, "core", SWAP)
    direction = assemble(pick, same, other)

    outer_rows = lax.dot_general(
        owned, owned, (((1,), (1,)), ((), ())), preferred_element_type=jnp.float32
    )
    outer_cols = lax.dot_general(
        owned, owned, (((0,), (0,)), ((), ())), preferred_element_type=jnp.float32
    )
    new_left = (decay * left_factor[0, 0] + (1.0 - decay) * outer_rows)[None, None]
    new_right = (decay * right_factor[0, 0] + (1.0 - decay) * outer_cols)[None, None]
    return (direction, new_left, new_right)


def solution(mesh):
    fine = Mesh(mesh.devices.reshape(NY, NX, NZ, NC, NT), ("y", "x", "zl", "core", "tensor"))
    owner = ("zl", "core")
    placed = (
        P(("y", "x") + owner, "tensor", None, None),
        P("tensor", None),
        P(owner, "tensor", None, None),
        P(owner, "tensor", None, None),
        P(owner, "tensor", None, None),
        P(owner, "tensor", None, None),
    )
    return jax.shard_map(
        local,
        mesh=fine,
        in_specs=placed,
        out_specs=(
            P("tensor", None, None),
            P(owner, "tensor", None, None),
            P(owner, "tensor", None, None),
        ),
        check_vma=False,
    )
```

```python
import jax
import jax.numpy as jnp
from jax import lax
from jax.experimental import pallas as pl
from jax.experimental.pallas import tpu as pltpu
from jax.sharding import Mesh, PartitionSpec as P

decay = 0.9
epsilon = 1e-06

NY, NX, NZ, NC, NT = 8, 4, 3, 2, 4
B = 512
ROWS = B // (NX * NY)
SWAP = [(0, 1), (1, 0)]


def add_up(terms):
    return jnp.sum(terms.astype(jnp.float32), axis=0).astype(jnp.bfloat16)


def place_kernel(count, where_ref, *refs):
    blocks, (out_ref, held, in_sem, out_sem) = refs[:count], refs[-4:]
    for i in range(count):
        pltpu.make_async_copy(blocks[i], held.at[i], in_sem.at[i]).start()
    for i in range(count):
        pltpu.make_async_copy(blocks[i], held.at[i], in_sem.at[i]).wait()
        pltpu.make_async_copy(held.at[i], out_ref.at[where_ref[i]], out_sem.at[i]).start()
    for i in range(count):
        pltpu.make_async_copy(held.at[i], out_ref.at[where_ref[i]], out_sem.at[i]).wait()


def place(where, blocks, into=None):
    count = len(blocks)
    extra = [] if into is None else [into]
    return pl.pallas_call(
        lambda *refs: place_kernel(count, *refs),
        out_shape=jax.ShapeDtypeStruct((NZ * NC, B, B), jnp.bfloat16),
        in_specs=[pl.BlockSpec(memory_space=pltpu.SMEM)]
        + [pl.BlockSpec(memory_space=pl.ANY)] * (count + len(extra)),
        out_specs=pl.BlockSpec(memory_space=pl.ANY),
        scratch_shapes=[
            pltpu.VMEM((count, B, B), jnp.bfloat16),
            pltpu.SemaphoreType.DMA((count,)),
            pltpu.SemaphoreType.DMA((count,)),
        ],
        input_output_aliases={1 + count: 0} if extra else {},
        cost_estimate=pl.CostEstimate(flops=0, bytes_accessed=4 * count * B * B, transcendentals=0),
        name="place",
    )(where, *blocks, *extra)


def local(grad_partial, owner_table, left_factor, right_factor, left_precond, right_precond):
    table_row = owner_table[0]
    core = lax.axis_index("core")
    height = lax.axis_index("zl")
    count = table_row.shape[0]
    positions = jnp.arange(count, dtype=jnp.int32)
    slot = positions % NZ
    side = jnp.where(positions < NZ, core, 1 - core)
    matches = table_row[None, :] == (2 * slot + side)[:, None]
    source = jnp.sum(jnp.where(matches, positions[None, :], 0), axis=1)
    behind = 2 * ((height - slot + NZ) % NZ) + side
    arrives = table_row[None, :] == behind[:, None]
    where = jnp.sum(jnp.where(arrives, positions[None, :], 0), axis=1)

    grad = grad_partial[0]
    keep = grad.at[source[:NZ]].get(mode="promise_in_bounds")
    give = grad.at[source[NZ:]].get(mode="promise_in_bounds")
    got = lax.ppermute(give, "core", SWAP)
    pair = (keep.astype(jnp.float32) + got.astype(jnp.float32)).astype(jnp.bfloat16)
    pieces = pair.reshape(NZ, NY, NX, ROWS, B).transpose(2, 1, 0, 3, 4)
    over_x = lax.all_to_all(pieces.reshape(NX, NY * NZ * ROWS, B), "x", 0, 0)
    part = add_up(over_x)
    over_yz = lax.all_to_all(part.reshape(NY * NZ, ROWS, B), ("y", "zl"), 0, 0)
    mine = add_up(over_yz)
    spread = lax.all_to_all(jnp.broadcast_to(mine[None], (NY * NX, ROWS, B)), ("y", "x"), 0, 0)
    owned = spread.reshape(B, B)

    half_product = jnp.dot(left_precond[0, 0], owned, preferred_element_type=jnp.float32).astype(
        jnp.bfloat16
    )
    full_product = jnp.dot(half_product, right_precond[0, 0], preferred_element_type=jnp.float32)
    scaled = (full_product * lax.rsqrt(jnp.mean(full_product * full_product) + epsilon)).astype(
        jnp.bfloat16
    )
    near = lax.ppermute(scaled, "zl", [(z, (z + 1) % NZ) for z in range(NZ)])
    far = lax.ppermute(scaled, "zl", [(z, (z + 2) % NZ) for z in range(NZ)])
    scaled_other = lax.ppermute(scaled, "core", SWAP)
    near_other = lax.ppermute(near, "core", SWAP)
    early = jnp.stack([where[0], where[1], where[3], where[4]])
    late = jnp.stack([where[2], where[5]])
    direction = place(early, [scaled, near, scaled_other, near_other])
    far_other = lax.ppermute(far, "core", SWAP)
    direction = place(late, [far, far_other], direction)

    outer_rows = lax.dot_general(
        owned, owned, (((1,), (1,)), ((), ())), preferred_element_type=jnp.float32
    )
    outer_cols = lax.dot_general(
        owned, owned, (((0,), (0,)), ((), ())), preferred_element_type=jnp.float32
    )
    new_left = (decay * left_factor[0, 0] + (1.0 - decay) * outer_rows)[None, None]
    new_right = (decay * right_factor[0, 0] + (1.0 - decay) * outer_cols)[None, None]
    return (direction, new_left, new_right)


def solution(mesh):
    fine = Mesh(mesh.devices.reshape(NY, NX, NZ, NC, NT), ("y", "x", "zl", "core", "tensor"))
    owner = ("zl", "core")
    placed = (
        P(("y", "x") + owner, "tensor", None, None),
        P("tensor", None),
        P(owner, "tensor", None, None),
        P(owner, "tensor", None, None),
        P(owner, "tensor", None, None),
        P(owner, "tensor", None, None),
    )
    return jax.shard_map(
        local,
        mesh=fine,
        in_specs=placed,
        out_specs=(
            P("tensor", None, None),
            P(owner, "tensor", None, None),
            P(owner, "tensor", None, None),
        ),
        check_vma=False,
    )
```

```python
import functools

import jax
import jax.numpy as jnp
from jax import lax
from jax.experimental import pallas as pl
from jax.experimental.pallas import tpu as pltpu
from jax.sharding import Mesh, PartitionSpec as P


decay = 0.9
epsilon = 1e-06

NY, NX, NZ, NC, NT = 8, 4, 3, 2, 4
B = 512
ROWS = B // (NX * NY)
SWAP = [(0, 1), (1, 0)]
VMEM = pltpu.MemorySpace.VMEM
HBM = pltpu.MemorySpace.HBM
SMEM = pltpu.MemorySpace.SMEM


def block_of(table_ref, owner):
    found = jnp.int32(0)
    for k in range(NZ * NC):
        found = jnp.where(table_ref[0, k] == owner, jnp.int32(k), found)
    return found


def call(kernel, out, scalars, arrays, scratch=(), cost=0, space=VMEM):
    held = [pltpu.with_memory_space_constraint(a, space) for a in arrays]
    return pl.pallas_call(
        kernel,
        out_shape=pltpu.VMEM(out, jnp.bfloat16),
        in_specs=[pl.BlockSpec(memory_space=SMEM)] * len(scalars)
        + [pl.BlockSpec(memory_space=space)] * len(arrays),
        out_specs=pl.BlockSpec(memory_space=VMEM),
        scratch_shapes=list(scratch),
        compiler_params=pltpu.CompilerParams(vmem_limit_bytes=2**22),
        cost_estimate=pl.CostEstimate(flops=0, bytes_accessed=cost, transcendentals=0),
    )(*scalars, *held)


def give_kernel(table_ref, place_ref, grad_ref, out_ref, sem):
    copies = [
        pltpu.make_async_copy(
            grad_ref.at[block_of(table_ref, 2 * z + 1 - place_ref[0])], out_ref.at[z], sem.at[z]
        )
        for z in range(NZ)
    ]
    for copy in copies:
        copy.start()
    for copy in copies:
        copy.wait()


def pair_kernel(table_ref, place_ref, grad_ref, got_ref, out_ref):
    for z in range(NZ):
        mine = block_of(table_ref, 2 * z + place_ref[0])
        for piece in range(NX * NY):
            rows = pl.ds(piece * ROWS, ROWS)
            total = grad_ref[mine, rows].astype(jnp.float32) + got_ref[z, rows].astype(jnp.float32)
            out_ref[piece % NX, piece // NX, z] = total.astype(out_ref.dtype)


def sum_kernel(terms_ref, out_ref):
    count, pieces = terms_ref.shape[0], terms_ref.shape[1]

    def step(i, carry):
        total = terms_ref[0, i].astype(jnp.float32)
        for t in range(1, count):
            total = total + terms_ref[t, i].astype(jnp.float32)
        out_ref[i] = total.astype(out_ref.dtype)
        return carry

    lax.fori_loop(0, pieces, step, 0, unroll=2)


def spread_kernel(terms_ref, out_ref):
    total = terms_ref[0].astype(jnp.float32)
    for t in range(1, terms_ref.shape[0]):
        total = total + terms_ref[t].astype(jnp.float32)
    strip = total.astype(out_ref.dtype)
    for i in range(out_ref.shape[0]):
        out_ref[i] = strip


def direction_kernel(left_ref, owned_ref, right_ref, out_ref, full_ref):
    step = 128
    square = jnp.zeros((8, 128), jnp.float32)
    for i in range(B // step):
        rows = pl.ds(i * step, step)
        half = jnp.dot(left_ref[rows], owned_ref[...], preferred_element_type=jnp.float32)
        full = jnp.dot(half.astype(jnp.bfloat16), right_ref[...], preferred_element_type=jnp.float32)
        full_ref[rows] = full
        square = square + jnp.sum((full * full).reshape(step // 8, 8, B // 128, 128), axis=(0, 2))
    scale = lax.rsqrt(jnp.sum(square) * (1.0 / (B * B)) + epsilon)
    for i in range(B // step):
        rows = pl.ds(i * step, step)
        out_ref[rows] = (full_ref[rows] * scale).astype(out_ref.dtype)


def place_kernel(hops, table_ref, place_ref, *refs):
    count = len(hops)
    blocks, out_ref, sem = refs[:count], refs[-2], refs[-1]
    copies = []
    for i, (d, s) in enumerate(hops):
        core = place_ref[0] if s == 0 else 1 - place_ref[0]
        z = lax.rem(place_ref[1] + NZ - d, jnp.int32(NZ))
        copies.append(
            pltpu.make_async_copy(blocks[i], out_ref.at[block_of(table_ref, 2 * z + core)], sem.at[i])
        )
    for copy in copies:
        copy.start()
    for copy in copies:
        copy.wait()


def place(table, here, hops, blocks, into=None):
    count = len(blocks)
    extra = [] if into is None else [into]
    held = [pltpu.with_memory_space_constraint(b, VMEM) for b in blocks]
    return pl.pallas_call(
        functools.partial(place_kernel, hops),
        out_shape=jax.ShapeDtypeStruct((NZ * NC, B, B), jnp.bfloat16),
        in_specs=[pl.BlockSpec(memory_space=SMEM)] * 2
        + [pl.BlockSpec(memory_space=VMEM)] * count
        + [pl.BlockSpec(memory_space=pl.ANY)] * len(extra),
        out_specs=pl.BlockSpec(memory_space=pl.ANY),
        scratch_shapes=[pltpu.SemaphoreType.DMA((count,))],
        input_output_aliases={2 + count: 0} if extra else {},
        compiler_params=pltpu.CompilerParams(vmem_limit_bytes=2**22),
        cost_estimate=pl.CostEstimate(flops=0, bytes_accessed=2 * count * B * B, transcendentals=0),
        name="place",
    )(table, here, *held, *extra)


def step(grad_partial, owner_table, left_factor, right_factor, left_precond, right_precond):
    core = lax.axis_index("core")
    here = jnp.stack([core, lax.axis_index("zl")]).astype(jnp.int32)

    give = call(
        give_kernel,
        (NZ, B, B),
        (owner_table, here),
        (grad_partial[0],),
        scratch=[pltpu.SemaphoreType.DMA((NZ,))],
        cost=2**21,
        space=HBM,
    )
    got = lax.ppermute(give, "core", SWAP)
    pieces = call(
        pair_kernel, (NX, NY, NZ, ROWS, B), (owner_table, here), (grad_partial[0], got), cost=2**22
    )
    over_x = lax.all_to_all(pieces.reshape(NX, NY * NZ, ROWS, B), "x", 0, 0)
    part = call(sum_kernel, (NY * NZ, ROWS, B), (), (over_x,), cost=2**21)
    over_yz = lax.all_to_all(part, ("y", "zl"), 0, 0)
    strips = call(spread_kernel, (NY * NX, ROWS, B), (), (over_yz,), cost=2**20)
    owned = lax.all_to_all(strips, ("y", "x"), 0, 0).reshape(B, B)

    scaled = call(
        direction_kernel,
        (B, B),
        (),
        (left_precond[0, 0], owned, right_precond[0, 0]),
        scratch=[pltpu.VMEM((B, B), jnp.float32)],
        cost=2**21,
    )
    near = lax.ppermute(scaled, "zl", [(z, (z + 1) % NZ) for z in range(NZ)])
    far = lax.ppermute(scaled, "zl", [(z, (z + 2) % NZ) for z in range(NZ)])
    scaled_other = lax.ppermute(scaled, "core", SWAP)
    near_other = lax.ppermute(near, "core", SWAP)
    early = [(0, 0), (1, 0), (0, 1), (1, 1)]
    direction = place(owner_table, here, early, [scaled, near, scaled_other, near_other])
    far_other = lax.ppermute(far, "core", SWAP)
    direction = place(owner_table, here, [(2, 0), (2, 1)], [far, far_other], direction)

    outer_rows = lax.dot_general(
        owned, owned, (((1,), (1,)), ((), ())), preferred_element_type=jnp.float32
    )
    new_left = (decay * left_factor[0, 0] + (1.0 - decay) * outer_rows)[None, None]
    outer_cols = lax.dot_general(
        owned, owned, (((0,), (0,)), ((), ())), preferred_element_type=jnp.float32
    )
    new_right = (decay * right_factor[0, 0] + (1.0 - decay) * outer_cols)[None, None]
    return (direction, new_left, new_right)


def solution(mesh):
    fine = Mesh(mesh.devices.reshape(NY, NX, NZ, NC, NT), ("y", "x", "zl", "core", "tensor"))
    owner = ("zl", "core")
    placed = (
        P(("y", "x") + owner, "tensor", None, None),
        P("tensor", None),
        P(owner, "tensor", None, None),
        P(owner, "tensor", None, None),
        P(owner, "tensor", None, None),
        P(owner, "tensor", None, None),
    )
    return jax.shard_map(
        step,
        mesh=fine,
        in_specs=placed,
        out_specs=(
            P("tensor", None, None),
            P(owner, "tensor", None, None),
            P(owner, "tensor", None, None),
        ),
        check_vma=False,
    )
```

```python
import functools

import jax
import jax.numpy as jnp
from jax import lax
from jax.experimental import pallas as pl
from jax.experimental.pallas import tpu as pltpu
from jax.sharding import Mesh, PartitionSpec as P


decay = 0.9
epsilon = 1e-06

NY, NX, NZ, NC, NT = 8, 4, 3, 2, 4
B = 512
ROWS = B // (NX * NY)
NEAR, AWAY = 4, 8
SWAP = [(0, 1), (1, 0)]
SLAB = ("y", "x", "zl", "core")
VMEM = pltpu.MemorySpace.VMEM
HBM = pltpu.MemorySpace.HBM
SMEM = pltpu.MemorySpace.SMEM


def device(core, height, quad, member):
    y = (2 * (quad // 2) + member // 2 + core) % NY
    x = (2 * (quad % 2) + member % 2 + core) % NX
    return ((y * NX + x) * NZ + height) * NC + core


QUADS = [[device(c, z, f, q) for q in range(NEAR)] for c in range(NC) for z in range(NZ) for f in range(AWAY)]
AWAYS = [[device(c, z, f, q) for f in range(AWAY)] for c in range(NC) for z in range(NZ) for q in range(NEAR)]
AWAY_Z = [
    [device(c, z, f, q) for f in range(AWAY) for z in range(NZ)] for c in range(NC) for q in range(NEAR)
]


def block_of(table_ref, owner):
    found = jnp.int32(0)
    for k in range(NZ * NC):
        found = jnp.where(table_ref[0, k] == owner, jnp.int32(k), found)
    return found


def call(kernel, out, scalars, arrays, scratch=(), cost=0, space=VMEM):
    held = [pltpu.with_memory_space_constraint(a, space) for a in arrays]
    return pl.pallas_call(
        kernel,
        out_shape=tuple(pltpu.VMEM(o, jnp.bfloat16) for o in out)
        if isinstance(out[0], tuple)
        else pltpu.VMEM(out, jnp.bfloat16),
        in_specs=[pl.BlockSpec(memory_space=SMEM)] * len(scalars)
        + [pl.BlockSpec(memory_space=space)] * len(arrays),
        out_specs=(pl.BlockSpec(memory_space=VMEM),) * len(out)
        if isinstance(out[0], tuple)
        else pl.BlockSpec(memory_space=VMEM),
        scratch_shapes=list(scratch),
        compiler_params=pltpu.CompilerParams(vmem_limit_bytes=2**22),
        cost_estimate=pl.CostEstimate(flops=0, bytes_accessed=cost, transcendentals=0),
    )(*scalars, *held)


def give_kernel(table_ref, place_ref, grad_ref, out_ref, sem):
    copies = [
        pltpu.make_async_copy(
            grad_ref.at[block_of(table_ref, 2 * z + 1 - place_ref[0])], out_ref.at[z], sem.at[z]
        )
        for z in range(NZ)
    ]
    for copy in copies:
        copy.start()
    for copy in copies:
        copy.wait()


def pair_kernel(table_ref, place_ref, grad_ref, got_ref, out_ref):
    for z in range(NZ):
        mine = block_of(table_ref, 2 * z + place_ref[0])
        for piece in range(NX * NY):
            rows = pl.ds(piece * ROWS, ROWS)
            total = grad_ref[mine, rows].astype(jnp.float32) + got_ref[z, rows].astype(jnp.float32)
            out_ref[piece // AWAY, piece % AWAY, z] = total.astype(out_ref.dtype)


def sum_kernel(terms_ref, out_ref):
    count, pieces = terms_ref.shape[0], terms_ref.shape[1]

    def step(i, carry):
        total = terms_ref[0, i].astype(jnp.float32)
        for t in range(1, count):
            total = total + terms_ref[t, i].astype(jnp.float32)
        out_ref[i] = total.astype(out_ref.dtype)
        return carry

    lax.fori_loop(0, pieces, step, 0, unroll=2)


def spread_kernel(terms_ref, out_ref):
    total = terms_ref[0].astype(jnp.float32)
    for t in range(1, terms_ref.shape[0]):
        total = total + terms_ref[t].astype(jnp.float32)
    strip = total.astype(out_ref.dtype)
    for i in range(out_ref.shape[0]):
        out_ref[i] = strip


def repeat_kernel(strip_ref, out_ref):
    for i in range(out_ref.shape[0]):
        out_ref[i] = strip_ref[...]


def foreign_kernel(place_ref, strips_ref, out_ref):
    for d in range(1, NZ):
        strip = strips_ref[lax.rem(place_ref[1] + NZ - d, jnp.int32(NZ))]
        for i in range(out_ref.shape[0]):
            out_ref[i, d - 1] = strip


def direction_kernel(place_ref, left_ref, owned_ref, right_ref, out_ref, strips_ref, full_ref):
    step = B // NEAR
    square = jnp.zeros((8, 128), jnp.float32)
    for i in range(NEAR):
        rows = pl.ds(i * step, step)
        half = jnp.dot(left_ref[rows], owned_ref[...], preferred_element_type=jnp.float32)
        full = jnp.dot(half.astype(jnp.bfloat16), right_ref[...], preferred_element_type=jnp.float32)
        full_ref[i] = full
        square = square + jnp.sum((full * full).reshape(step // 8, 8, B // 128, 128), axis=(0, 2))
    scale = lax.rsqrt(jnp.sum(square) * (1.0 / (B * B)) + epsilon)
    for i in range(NEAR):
        out_ref[i] = (full_ref[i] * scale).astype(out_ref.dtype)
    strip = out_ref[place_ref[2]]
    for z in range(NZ):
        strips_ref[z] = strip


def place_kernel(parts, table_ref, place_ref, *refs):
    out_ref, sem = refs[-2], refs[-1]
    copies = []
    for n, (i, d, s) in enumerate(parts):
        core = place_ref[0] if s == 0 else 1 - place_ref[0]
        z = lax.rem(place_ref[1] + NZ - d, jnp.int32(NZ))
        block = refs[i] if d == 0 else refs[i].at[:, d - 1]
        to = out_ref.at[block_of(table_ref, 2 * z + core)]
        copies.append(pltpu.make_async_copy(block, to, sem.at[n]))
    for copy in copies:
        copy.start()
    for copy in copies:
        copy.wait()


def place(table, here, parts, arrays, into=None):
    count = len(arrays)
    extra = [] if into is None else [into]
    held = [pltpu.with_memory_space_constraint(a, VMEM) for a in arrays]
    return pl.pallas_call(
        functools.partial(place_kernel, parts),
        out_shape=jax.ShapeDtypeStruct((NZ * NC, NEAR, B // NEAR, B), jnp.bfloat16),
        in_specs=[pl.BlockSpec(memory_space=SMEM)] * 2
        + [pl.BlockSpec(memory_space=VMEM)] * count
        + [pl.BlockSpec(memory_space=pl.ANY)] * len(extra),
        out_specs=pl.BlockSpec(memory_space=pl.ANY),
        scratch_shapes=[pltpu.SemaphoreType.DMA((len(parts),))],
        input_output_aliases={2 + count: 0} if extra else {},
        compiler_params=pltpu.CompilerParams(vmem_limit_bytes=2**22),
        cost_estimate=pl.CostEstimate(flops=0, bytes_accessed=2 * len(parts) * B * B, transcendentals=0),
        name="place",
    )(table, here, *held, *extra)


def exchange(pieces, groups):
    return lax.all_to_all(pieces, SLAB, 0, 0, axis_index_groups=groups)


def step(grad_partial, owner_table, left_factor, right_factor, left_precond, right_precond):
    core = lax.axis_index("core")
    quarter = 2 * ((lax.axis_index("y") + core) % 2) + (lax.axis_index("x") + core) % 2
    here = jnp.stack([core, lax.axis_index("zl"), quarter]).astype(jnp.int32)

    give = call(
        give_kernel,
        (NZ, B, B),
        (owner_table, here),
        (grad_partial[0],),
        scratch=[pltpu.SemaphoreType.DMA((NZ,))],
        cost=2**21,
        space=HBM,
    )
    got = lax.ppermute(give, "core", SWAP)
    pieces = call(pair_kernel, (NEAR, AWAY, NZ, ROWS, B), (owner_table, here), (grad_partial[0], got), cost=2**22)
    in_quad = exchange(pieces.reshape(NEAR, AWAY * NZ, ROWS, B), QUADS)
    part = call(sum_kernel, (AWAY * NZ, ROWS, B), (), (in_quad,), cost=2**21)
    strips = call(spread_kernel, (AWAY, ROWS, B), (), (exchange(part, AWAY_Z),), cost=2**20)
    strip = exchange(strips, AWAYS).reshape(B // NEAR, B)
    strips = call(repeat_kernel, (NEAR, B // NEAR, B), (), (strip,), cost=2**20)
    owned = exchange(strips, QUADS).reshape(B, B)

    scaled, strips = call(
        direction_kernel,
        ((NEAR, B // NEAR, B), (NZ, B // NEAR, B)),
        (here,),
        (left_precond[0, 0], owned, right_precond[0, 0]),
        scratch=[pltpu.VMEM((NEAR, B // NEAR, B), jnp.float32)],
        cost=2**21,
    )
    scaled_other = lax.ppermute(scaled, "core", SWAP)
    strips = lax.all_to_all(strips, "zl", 0, 0)
    foreign = call(foreign_kernel, (NEAR, NZ - 1, B // NEAR, B), (here,), (strips,), cost=2**20)
    foreign = exchange(foreign, QUADS)
    direction = place(owner_table, here, [(0, 0, 0), (1, 0, 1)], [scaled, scaled_other])
    foreign_other = lax.ppermute(foreign, "core", SWAP)
    late = [(0, 1, 0), (0, 2, 0), (1, 1, 1), (1, 2, 1)]
    direction = place(owner_table, here, late, [foreign, foreign_other], direction).reshape(NZ * NC, B, B)

    outer_rows = lax.dot_general(
        owned, owned, (((1,), (1,)), ((), ())), preferred_element_type=jnp.float32
    )
    new_left = (decay * left_factor[0, 0] + (1.0 - decay) * outer_rows)[None, None]
    outer_cols = lax.dot_general(
        owned, owned, (((0,), (0,)), ((), ())), preferred_element_type=jnp.float32
    )
    new_right = (decay * right_factor[0, 0] + (1.0 - decay) * outer_cols)[None, None]
    return (direction, new_left, new_right)


def solution(mesh):
    fine = Mesh(mesh.devices.reshape(NY, NX, NZ, NC, NT), ("y", "x", "zl", "core", "tensor"))
    owner = ("zl", "core")
    placed = (
        P(("y", "x") + owner, "tensor", None, None),
        P("tensor", None),
        P(owner, "tensor", None, None),
        P(owner, "tensor", None, None),
        P(owner, "tensor", None, None),
        P(owner, "tensor", None, None),
    )
    return jax.shard_map(
        step,
        mesh=fine,
        in_specs=placed,
        out_specs=(
            P("tensor", None, None),
            P(owner, "tensor", None, None),
            P(owner, "tensor", None, None),
        ),
        check_vma=False,
    )
```

```python
import functools

import jax
import jax.numpy as jnp
from jax import lax
from jax.experimental import pallas as pl
from jax.experimental.pallas import tpu as pltpu
from jax.sharding import Mesh, PartitionSpec as P


decay = 0.9
epsilon = 1e-06

NY, NX, NZ, NC, NT = 8, 4, 3, 2, 4
B = 512
ROWS = B // (NX * NY)
NEAR, AWAY = 4, 8
SWAP = [(0, 1), (1, 0)]
SLAB = ("y", "x", "zl", "core")
VMEM = pltpu.MemorySpace.VMEM
HBM = pltpu.MemorySpace.HBM
SMEM = pltpu.MemorySpace.SMEM


def device(core, height, quad, member):
    y = (2 * (quad // 2) + member // 2 + core) % NY
    x = (2 * (quad % 2) + member % 2 + core) % NX
    return ((y * NX + x) * NZ + height) * NC + core


QUADS = [[device(c, z, f, q) for q in range(NEAR)] for c in range(NC) for z in range(NZ) for f in range(AWAY)]
PLANES = [
    [device(c, z, f, q) for q in range(NEAR) for f in range(AWAY)] for c in range(NC) for z in range(NZ)
]
AWAY_Z = [
    [device(c, z, f, q) for f in range(AWAY) for z in range(NZ)] for c in range(NC) for q in range(NEAR)
]


def block_of(table_ref, owner):
    found = jnp.int32(0)
    for k in range(NZ * NC):
        found = jnp.where(table_ref[0, k] == owner, jnp.int32(k), found)
    return found


def call(kernel, out, scalars, arrays, scratch=(), cost=0, space=VMEM):
    held = [pltpu.with_memory_space_constraint(a, space) for a in arrays]
    return pl.pallas_call(
        kernel,
        out_shape=tuple(pltpu.VMEM(o, jnp.bfloat16) for o in out)
        if isinstance(out[0], tuple)
        else pltpu.VMEM(out, jnp.bfloat16),
        in_specs=[pl.BlockSpec(memory_space=SMEM)] * len(scalars)
        + [pl.BlockSpec(memory_space=space)] * len(arrays),
        out_specs=(pl.BlockSpec(memory_space=VMEM),) * len(out)
        if isinstance(out[0], tuple)
        else pl.BlockSpec(memory_space=VMEM),
        scratch_shapes=list(scratch),
        compiler_params=pltpu.CompilerParams(vmem_limit_bytes=2**22),
        cost_estimate=pl.CostEstimate(flops=0, bytes_accessed=cost, transcendentals=0),
    )(*scalars, *held)


def give_kernel(table_ref, place_ref, grad_ref, out_ref, sem):
    copies = [
        pltpu.make_async_copy(
            grad_ref.at[block_of(table_ref, 2 * z + 1 - place_ref[0])], out_ref.at[z], sem.at[z]
        )
        for z in range(NZ)
    ]
    for copy in copies:
        copy.start()
    for copy in copies:
        copy.wait()


def pair_kernel(table_ref, place_ref, grad_ref, got_ref, out_ref):
    for z in range(NZ):
        mine = block_of(table_ref, 2 * z + place_ref[0])
        for piece in range(NX * NY):
            rows = pl.ds(piece * ROWS, ROWS)
            total = grad_ref[mine, rows].astype(jnp.float32) + got_ref[z, rows].astype(jnp.float32)
            out_ref[piece // AWAY, piece % AWAY, z] = total.astype(out_ref.dtype)


def sum_kernel(terms_ref, out_ref):
    count, pieces = terms_ref.shape[0], terms_ref.shape[1]

    def step(i, carry):
        total = terms_ref[0, i].astype(jnp.float32)
        for t in range(1, count):
            total = total + terms_ref[t, i].astype(jnp.float32)
        out_ref[i] = total.astype(out_ref.dtype)
        return carry

    lax.fori_loop(0, pieces, step, 0, unroll=2)


def spread_kernel(terms_ref, out_ref):
    total = terms_ref[0].astype(jnp.float32)
    for t in range(1, terms_ref.shape[0]):
        total = total + terms_ref[t].astype(jnp.float32)
    strip = total.astype(out_ref.dtype)
    for i in range(out_ref.shape[0]):
        out_ref[i] = strip


def foreign_kernel(place_ref, strips_ref, out_ref):
    for d in range(1, NZ):
        strip = strips_ref[lax.rem(place_ref[1] + NZ - d, jnp.int32(NZ))]
        for i in range(out_ref.shape[0]):
            out_ref[i, d - 1] = strip


def direction_kernel(place_ref, left_ref, owned_ref, right_ref, out_ref, strips_ref, full_ref):
    step = B // NEAR
    square = jnp.zeros((8, 128), jnp.float32)
    for i in range(NEAR):
        rows = pl.ds(i * step, step)
        half = jnp.dot(left_ref[rows], owned_ref[...], preferred_element_type=jnp.float32)
        full = jnp.dot(half.astype(jnp.bfloat16), right_ref[...], preferred_element_type=jnp.float32)
        full_ref[i] = full
        square = square + jnp.sum((full * full).reshape(step // 8, 8, B // 128, 128), axis=(0, 2))
    scale = lax.rsqrt(jnp.sum(square) * (1.0 / (B * B)) + epsilon)
    for i in range(NEAR):
        out_ref[i] = (full_ref[i] * scale).astype(out_ref.dtype)
    strip = out_ref[place_ref[2]]
    for z in range(NZ):
        strips_ref[z] = strip


def place_kernel(parts, table_ref, place_ref, *refs):
    out_ref, sem = refs[-2], refs[-1]
    copies = []
    for n, (i, d, s) in enumerate(parts):
        core = place_ref[0] if s == 0 else 1 - place_ref[0]
        z = lax.rem(place_ref[1] + NZ - d, jnp.int32(NZ))
        block = refs[i] if d == 0 else refs[i].at[:, d - 1]
        to = out_ref.at[block_of(table_ref, 2 * z + core)]
        copies.append(pltpu.make_async_copy(block, to, sem.at[n]))
    for copy in copies:
        copy.start()
    for copy in copies:
        copy.wait()


def place(table, here, parts, arrays, into=None):
    count = len(arrays)
    extra = [] if into is None else [into]
    held = [pltpu.with_memory_space_constraint(a, VMEM) for a in arrays]
    return pl.pallas_call(
        functools.partial(place_kernel, parts),
        out_shape=jax.ShapeDtypeStruct((NZ * NC, NEAR, B // NEAR, B), jnp.bfloat16),
        in_specs=[pl.BlockSpec(memory_space=SMEM)] * 2
        + [pl.BlockSpec(memory_space=VMEM)] * count
        + [pl.BlockSpec(memory_space=pl.ANY)] * len(extra),
        out_specs=pl.BlockSpec(memory_space=pl.ANY),
        scratch_shapes=[pltpu.SemaphoreType.DMA((len(parts),))],
        input_output_aliases={2 + count: 0} if extra else {},
        compiler_params=pltpu.CompilerParams(vmem_limit_bytes=2**22),
        cost_estimate=pl.CostEstimate(flops=0, bytes_accessed=2 * len(parts) * B * B, transcendentals=0),
        name="place",
    )(table, here, *held, *extra)


def exchange(pieces, groups):
    return lax.all_to_all(pieces, SLAB, 0, 0, axis_index_groups=groups)


def step(grad_partial, owner_table, left_factor, right_factor, left_precond, right_precond):
    core = lax.axis_index("core")
    quarter = 2 * ((lax.axis_index("y") + core) % 2) + (lax.axis_index("x") + core) % 2
    here = jnp.stack([core, lax.axis_index("zl"), quarter]).astype(jnp.int32)

    give = call(
        give_kernel,
        (NZ, B, B),
        (owner_table, here),
        (grad_partial[0],),
        scratch=[pltpu.SemaphoreType.DMA((NZ,))],
        cost=2**21,
        space=HBM,
    )
    got = lax.ppermute(give, "core", SWAP)
    pieces = call(pair_kernel, (NEAR, AWAY, NZ, ROWS, B), (owner_table, here), (grad_partial[0], got), cost=2**22)
    in_quad = exchange(pieces.reshape(NEAR, AWAY * NZ, ROWS, B), QUADS)
    part = call(sum_kernel, (AWAY * NZ, ROWS, B), (), (in_quad,), cost=2**21)
    strips = call(spread_kernel, (NEAR * AWAY, ROWS, B), (), (exchange(part, AWAY_Z),), cost=2**20)
    owned = exchange(strips, PLANES).reshape(B, B)

    scaled, strips = call(
        direction_kernel,
        ((NEAR, B // NEAR, B), (NZ, B // NEAR, B)),
        (here,),
        (left_precond[0, 0], owned, right_precond[0, 0]),
        scratch=[pltpu.VMEM((NEAR, B // NEAR, B), jnp.float32)],
        cost=2**21,
    )
    scaled_other = lax.ppermute(scaled, "core", SWAP)
    strips = lax.all_to_all(strips, "zl", 0, 0)
    direction = place(owner_table, here, [(0, 0, 0), (1, 0, 1)], [scaled, scaled_other])
    foreign = call(foreign_kernel, (NEAR, NZ - 1, B // NEAR, B), (here,), (strips,), cost=2**20)
    foreign = exchange(foreign, QUADS)
    foreign_other = lax.ppermute(foreign, "core", SWAP)
    late = [(0, 1, 0), (0, 2, 0), (1, 1, 1), (1, 2, 1)]
    direction = place(owner_table, here, late, [foreign, foreign_other], direction).reshape(NZ * NC, B, B)

    outer_rows = lax.dot_general(
        owned, owned, (((1,), (1,)), ((), ())), preferred_element_type=jnp.float32
    )
    new_left = (decay * left_factor[0, 0] + (1.0 - decay) * outer_rows)[None, None]
    outer_cols = lax.dot_general(
        owned, owned, (((0,), (0,)), ((), ())), preferred_element_type=jnp.float32
    )
    new_right = (decay * right_factor[0, 0] + (1.0 - decay) * outer_cols)[None, None]
    return (direction, new_left, new_right)


def solution(mesh):
    fine = Mesh(mesh.devices.reshape(NY, NX, NZ, NC, NT), ("y", "x", "zl", "core", "tensor"))
    owner = ("zl", "core")
    placed = (
        P(("y", "x") + owner, "tensor", None, None),
        P("tensor", None),
        P(owner, "tensor", None, None),
        P(owner, "tensor", None, None),
        P(owner, "tensor", None, None),
        P(owner, "tensor", None, None),
    )
    return jax.shard_map(
        step,
        mesh=fine,
        in_specs=placed,
        out_specs=(
            P("tensor", None, None),
            P(owner, "tensor", None, None),
            P(owner, "tensor", None, None),
        ),
        check_vma=False,
    )
```

```python
import functools

import jax
import jax.numpy as jnp
from jax import lax
from jax.experimental import pallas as pl
from jax.experimental.pallas import tpu as pltpu
from jax.sharding import Mesh, PartitionSpec as P


decay = 0.9
epsilon = 1e-06

NY, NX, NZ, NC, NT = 8, 4, 3, 2, 4
B = 512
ROWS = B // (NX * NY)
NEAR, AWAY = 4, 8
SWAP = [(0, 1), (1, 0)]
SLAB = ("y", "x", "zl", "core")
VMEM = pltpu.MemorySpace.VMEM
HBM = pltpu.MemorySpace.HBM
SMEM = pltpu.MemorySpace.SMEM


def device(core, height, quad, member):
    y = (2 * (quad // 2) + member // 2 + core) % NY
    x = (2 * (quad % 2) + member % 2 + core) % NX
    return ((y * NX + x) * NZ + height) * NC + core


QUADS = [[device(c, z, f, q) for q in range(NEAR)] for c in range(NC) for z in range(NZ) for f in range(AWAY)]
AWAY_Z = [
    [device(c, z, f, q) for f in range(AWAY) for z in range(NZ)] for c in range(NC) for q in range(NEAR)
]


def block_of(info_ref, owner):
    found = jnp.int32(0)
    for k in range(NZ * NC):
        found = jnp.where(info_ref[3 + k] == owner, jnp.int32(k), found)
    return found


def call(kernel, out, scalars, arrays, scratch=(), cost=0, space=VMEM):
    held = [pltpu.with_memory_space_constraint(a, space) for a in arrays]
    return pl.pallas_call(
        kernel,
        out_shape=tuple(pltpu.VMEM(o, jnp.bfloat16) for o in out)
        if isinstance(out[0], tuple)
        else pltpu.VMEM(out, jnp.bfloat16),
        in_specs=[pl.BlockSpec(memory_space=SMEM)] * len(scalars)
        + [pl.BlockSpec(memory_space=space)] * len(arrays),
        out_specs=(pl.BlockSpec(memory_space=VMEM),) * len(out)
        if isinstance(out[0], tuple)
        else pl.BlockSpec(memory_space=VMEM),
        scratch_shapes=list(scratch),
        compiler_params=pltpu.CompilerParams(vmem_limit_bytes=2**22),
        cost_estimate=pl.CostEstimate(flops=0, bytes_accessed=cost, transcendentals=0),
    )(*scalars, *held)


def fetch_kernel(other, info_ref, grad_ref, out_ref, sem):
    core = 1 - info_ref[0] if other else info_ref[0]
    copies = [
        pltpu.make_async_copy(grad_ref.at[block_of(info_ref, 2 * z + core)], out_ref.at[z], sem.at[z])
        for z in range(NZ)
    ]
    for copy in copies:
        copy.start()
    for copy in copies:
        copy.wait()


def pair_kernel(info_ref, keep_ref, got_ref, out_ref):
    core = info_ref[0]
    for y in range(NY):
        for x in range(NX):
            up, right = lax.rem(y + NY - core, jnp.int32(NY)), lax.rem(x + NX - core, jnp.int32(NX))
            member = 2 * lax.rem(up, jnp.int32(2)) + lax.rem(right, jnp.int32(2))
            quad = 2 * (up >> 1) + (right >> 1)
            rows = pl.ds((y * NX + x) * ROWS, ROWS)
            for z in range(NZ):
                total = keep_ref[z, rows].astype(jnp.float32) + got_ref[z, rows].astype(jnp.float32)
                out_ref[member, quad, z] = total.astype(out_ref.dtype)


def sum_kernel(terms_ref, out_ref):
    count, pieces = terms_ref.shape[0], terms_ref.shape[1]

    def step(i, carry):
        total = terms_ref[0, i].astype(jnp.float32)
        for t in range(1, count):
            total = total + terms_ref[t, i].astype(jnp.float32)
        out_ref[i] = total.astype(out_ref.dtype)
        return carry

    lax.fori_loop(0, pieces, step, 0, unroll=2)


def spread_kernel(terms_ref, out_ref):
    total = terms_ref[0].astype(jnp.float32)
    for t in range(1, terms_ref.shape[0]):
        total = total + terms_ref[t].astype(jnp.float32)
    strip = total.astype(out_ref.dtype)
    for i in range(out_ref.shape[0]):
        out_ref[i] = strip


def foreign_kernel(info_ref, strips_ref, out_ref):
    for d in range(1, NZ):
        strip = strips_ref[lax.rem(info_ref[1] + NZ - d, jnp.int32(NZ))]
        for i in range(out_ref.shape[0]):
            out_ref[i, d - 1] = strip


def direction_kernel(info_ref, left_ref, owned_ref, right_ref, out_ref, strips_ref, full_ref):
    step = B // NEAR
    square = jnp.zeros((8, 128), jnp.float32)
    for i in range(NEAR):
        rows = pl.ds(i * step, step)
        half = jnp.dot(left_ref[rows], owned_ref[...], preferred_element_type=jnp.float32)
        full = jnp.dot(half.astype(jnp.bfloat16), right_ref[...], preferred_element_type=jnp.float32)
        full_ref[i] = full
        square = square + jnp.sum((full * full).reshape(step // 8, 8, B // 128, 128), axis=(0, 2))
    scale = lax.rsqrt(jnp.sum(square) * (1.0 / (B * B)) + epsilon)
    for i in range(NEAR):
        out_ref[i] = (full_ref[i] * scale).astype(out_ref.dtype)
    strip = out_ref[info_ref[2]]
    for z in range(NZ):
        strips_ref[z] = strip


def place_kernel(parts, info_ref, *refs):
    out_ref, sem = refs[-2], refs[-1]
    copies = []
    for n, (i, d, s) in enumerate(parts):
        core = info_ref[0] if s == 0 else 1 - info_ref[0]
        z = lax.rem(info_ref[1] + NZ - d, jnp.int32(NZ))
        block = refs[i] if d == 0 else refs[i].at[:, d - 1]
        to = out_ref.at[block_of(info_ref, 2 * z + core)]
        copies.append(pltpu.make_async_copy(block, to, sem.at[n]))
    for copy in copies:
        copy.start()
    for copy in copies:
        copy.wait()


def place(info, parts, arrays, into=None):
    count = len(arrays)
    extra = [] if into is None else [into]
    held = [pltpu.with_memory_space_constraint(a, VMEM) for a in arrays]
    return pl.pallas_call(
        functools.partial(place_kernel, parts),
        out_shape=jax.ShapeDtypeStruct((NZ * NC, NEAR, B // NEAR, B), jnp.bfloat16),
        in_specs=[pl.BlockSpec(memory_space=SMEM)]
        + [pl.BlockSpec(memory_space=VMEM)] * count
        + [pl.BlockSpec(memory_space=pl.ANY)] * len(extra),
        out_specs=pl.BlockSpec(memory_space=pl.ANY),
        scratch_shapes=[pltpu.SemaphoreType.DMA((len(parts),))],
        input_output_aliases={1 + count: 0} if extra else {},
        compiler_params=pltpu.CompilerParams(vmem_limit_bytes=2**22),
        cost_estimate=pl.CostEstimate(flops=0, bytes_accessed=2 * len(parts) * B * B, transcendentals=0),
        name="place",
    )(info, *held, *extra)


def exchange(pieces, groups):
    return lax.all_to_all(pieces, SLAB, 0, 0, axis_index_groups=groups)


def step(grad_partial, owner_table, left_factor, right_factor, left_precond, right_precond):
    core = lax.axis_index("core")
    quarter = 2 * ((lax.axis_index("y") + core) % 2) + (lax.axis_index("x") + core) % 2
    here = jnp.stack([core, lax.axis_index("zl"), quarter]).astype(jnp.int32)
    info = jnp.concatenate([here, owner_table[0]])

    def fetch(other):
        return call(
            functools.partial(fetch_kernel, other),
            (NZ, B, B),
            (info,),
            (grad_partial[0],),
            scratch=[pltpu.SemaphoreType.DMA((NZ,))],
            cost=2**21,
            space=HBM,
        )

    give = fetch(True)
    got = lax.ppermute(give, "core", SWAP)
    keep = fetch(False)
    pieces = call(pair_kernel, (NEAR, AWAY, NZ, ROWS, B), (info,), (keep, got), cost=2**22)
    in_quad = exchange(pieces.reshape(NEAR, AWAY * NZ, ROWS, B), QUADS)
    part = call(sum_kernel, (AWAY * NZ, ROWS, B), (), (in_quad,), cost=2**21)
    strips = call(spread_kernel, (NEAR * AWAY, ROWS, B), (), (exchange(part, AWAY_Z),), cost=2**20)
    owned = lax.all_to_all(strips, ("y", "x"), 0, 0).reshape(B, B)

    scaled, strips = call(
        direction_kernel,
        ((NEAR, B // NEAR, B), (NZ, B // NEAR, B)),
        (info,),
        (left_precond[0, 0], owned, right_precond[0, 0]),
        scratch=[pltpu.VMEM((NEAR, B // NEAR, B), jnp.float32)],
        cost=2**21,
    )
    scaled_other = lax.ppermute(scaled, "core", SWAP)
    strips = lax.all_to_all(strips, "zl", 0, 0)
    direction = place(info, [(0, 0, 0), (1, 0, 1)], [scaled, scaled_other])
    foreign = call(foreign_kernel, (NEAR, NZ - 1, B // NEAR, B), (info,), (strips,), cost=2**20)
    foreign = exchange(foreign, QUADS)
    foreign_other = lax.ppermute(foreign, "core", SWAP)
    late = [(0, 1, 0), (0, 2, 0), (1, 1, 1), (1, 2, 1)]
    direction = place(info, late, [foreign, foreign_other], direction).reshape(NZ * NC, B, B)

    outer_rows = lax.dot_general(
        owned, owned, (((1,), (1,)), ((), ())), preferred_element_type=jnp.float32
    )
    new_left = (decay * left_factor[0, 0] + (1.0 - decay) * outer_rows)[None, None]
    outer_cols = lax.dot_general(
        owned, owned, (((0,), (0,)), ((), ())), preferred_element_type=jnp.float32
    )
    new_right = (decay * right_factor[0, 0] + (1.0 - decay) * outer_cols)[None, None]
    return (direction, new_left, new_right)


def solution(mesh):
    fine = Mesh(mesh.devices.reshape(NY, NX, NZ, NC, NT), ("y", "x", "zl", "core", "tensor"))
    owner = ("zl", "core")
    placed = (
        P(("y", "x") + owner, "tensor", None, None),
        P("tensor", None),
        P(owner, "tensor", None, None),
        P(owner, "tensor", None, None),
        P(owner, "tensor", None, None),
        P(owner, "tensor", None, None),
    )
    return jax.shard_map(
        step,
        mesh=fine,
        in_specs=placed,
        out_specs=(
            P("tensor", None, None),
            P(owner, "tensor", None, None),
            P(owner, "tensor", None, None),
        ),
        check_vma=False,
    )
```

```python
import functools

import jax
import jax.numpy as jnp
from jax import lax
from jax.experimental import pallas as pl
from jax.experimental.pallas import tpu as pltpu
from jax.sharding import Mesh, PartitionSpec as P


decay = 0.9
epsilon = 1e-06

NY, NX, NZ, NC, NT = 8, 4, 3, 2, 4
B = 512
ROWS = B // (NX * NY)
NEAR, AWAY = 4, 8
SWAP = [(0, 1), (1, 0)]
SLAB = ("y", "x", "zl", "core")
VMEM = pltpu.MemorySpace.VMEM
HBM = pltpu.MemorySpace.HBM
SMEM = pltpu.MemorySpace.SMEM


def device(core, height, quad, member):
    y = (2 * (quad // 2) + member // 2 + core) % NY
    x = (2 * (quad % 2) + member % 2 + core) % NX
    return ((y * NX + x) * NZ + height) * NC + core


QUADS = [[device(c, z, f, q) for q in range(NEAR)] for c in range(NC) for z in range(NZ) for f in range(AWAY)]
AWAY_Z = [
    [device(c, z, f, q) for f in range(AWAY) for z in range(NZ)] for c in range(NC) for q in range(NEAR)
]


def block_of(info_ref, owner):
    found = jnp.int32(0)
    for k in range(NZ * NC):
        found = jnp.where(info_ref[3 + k] == owner, jnp.int32(k), found)
    return found


def call(kernel, out, scalars, arrays, scratch=(), cost=0, space=VMEM):
    held = [pltpu.with_memory_space_constraint(a, space) for a in arrays]
    return pl.pallas_call(
        kernel,
        out_shape=tuple(pltpu.VMEM(o, jnp.bfloat16) for o in out)
        if isinstance(out[0], tuple)
        else pltpu.VMEM(out, jnp.bfloat16),
        in_specs=[pl.BlockSpec(memory_space=SMEM)] * len(scalars)
        + [pl.BlockSpec(memory_space=space)] * len(arrays),
        out_specs=(pl.BlockSpec(memory_space=VMEM),) * len(out)
        if isinstance(out[0], tuple)
        else pl.BlockSpec(memory_space=VMEM),
        scratch_shapes=list(scratch),
        compiler_params=pltpu.CompilerParams(vmem_limit_bytes=2**22),
        cost_estimate=pl.CostEstimate(flops=0, bytes_accessed=cost, transcendentals=0),
    )(*scalars, *held)


def fetch_kernel(other, info_ref, grad_ref, out_ref, sem):
    core = 1 - info_ref[0] if other else info_ref[0]
    copies = [
        pltpu.make_async_copy(grad_ref.at[block_of(info_ref, 2 * z + core)], out_ref.at[z], sem.at[z])
        for z in range(NZ)
    ]
    for copy in copies:
        copy.start()
    for copy in copies:
        copy.wait()


def pair_kernel(info_ref, keep_ref, got_ref, out_ref):
    core = info_ref[0]
    for y in range(NY):
        for x in range(NX):
            up, right = lax.rem(y + NY - core, jnp.int32(NY)), lax.rem(x + NX - core, jnp.int32(NX))
            member = 2 * lax.rem(up, jnp.int32(2)) + lax.rem(right, jnp.int32(2))
            quad = 2 * (up >> 1) + (right >> 1)
            rows = pl.ds((y * NX + x) * ROWS, ROWS)
            for z in range(NZ):
                total = keep_ref[z, rows].astype(jnp.float32) + got_ref[z, rows].astype(jnp.float32)
                out_ref[member, quad, z] = total.astype(out_ref.dtype)


def sum_kernel(terms_ref, out_ref):
    count, pieces = terms_ref.shape[0], terms_ref.shape[1]

    def step(i, carry):
        total = terms_ref[0, i].astype(jnp.float32)
        for t in range(1, count):
            total = total + terms_ref[t, i].astype(jnp.float32)
        out_ref[i] = total.astype(out_ref.dtype)
        return carry

    lax.fori_loop(0, pieces, step, 0, unroll=2)


def spread_kernel(terms_ref, out_ref):
    total = terms_ref[0].astype(jnp.float32)
    for t in range(1, terms_ref.shape[0]):
        total = total + terms_ref[t].astype(jnp.float32)
    strip = total.astype(out_ref.dtype)
    for i in range(out_ref.shape[0]):
        out_ref[i] = strip


def foreign_kernel(info_ref, strips_ref, out_ref):
    for d in range(1, NZ):
        strip = strips_ref[lax.rem(info_ref[1] + NZ - d, jnp.int32(NZ))]
        for i in range(out_ref.shape[0]):
            out_ref[i, d - 1] = strip


def direction_kernel(info_ref, left_ref, owned_ref, right_ref, out_ref, strips_ref, full_ref, strip_ref, sem):
    step = B // NEAR
    square = jnp.zeros((8, 128), jnp.float32)
    for i in range(NEAR):
        rows = pl.ds(i * step, step)
        half = jnp.dot(left_ref[rows], owned_ref[...], preferred_element_type=jnp.float32)
        full = jnp.dot(half.astype(jnp.bfloat16), right_ref[...], preferred_element_type=jnp.float32)
        full_ref[i] = full
        square = square + jnp.sum((full * full).reshape(step // 8, 8, B // 128, 128), axis=(0, 2))
    scale = lax.rsqrt(jnp.sum(square) * (1.0 / (B * B)) + epsilon)
    strip_ref[...] = (full_ref[info_ref[2]] * scale).astype(strip_ref.dtype)
    copies = [pltpu.make_async_copy(strip_ref, strips_ref.at[z], sem.at[z]) for z in range(NZ)]
    for copy in copies:
        copy.start()
    for i in range(NEAR):
        out_ref[i] = (full_ref[i] * scale).astype(out_ref.dtype)
    for copy in copies:
        copy.wait()


def place_kernel(parts, info_ref, *refs):
    out_ref, sem = refs[-2], refs[-1]
    copies = []
    for n, (i, d, s) in enumerate(parts):
        core = info_ref[0] if s == 0 else 1 - info_ref[0]
        z = lax.rem(info_ref[1] + NZ - d, jnp.int32(NZ))
        block = refs[i] if d == 0 else refs[i].at[:, d - 1]
        to = out_ref.at[block_of(info_ref, 2 * z + core)]
        copies.append(pltpu.make_async_copy(block, to, sem.at[n]))
    for copy in copies:
        copy.start()
    for copy in copies:
        copy.wait()


def place(info, parts, arrays, into=None):
    count = len(arrays)
    extra = [] if into is None else [into]
    held = [pltpu.with_memory_space_constraint(a, VMEM) for a in arrays]
    return pl.pallas_call(
        functools.partial(place_kernel, parts),
        out_shape=jax.ShapeDtypeStruct((NZ * NC, NEAR, B // NEAR, B), jnp.bfloat16),
        in_specs=[pl.BlockSpec(memory_space=SMEM)]
        + [pl.BlockSpec(memory_space=VMEM)] * count
        + [pl.BlockSpec(memory_space=pl.ANY)] * len(extra),
        out_specs=pl.BlockSpec(memory_space=pl.ANY),
        scratch_shapes=[pltpu.SemaphoreType.DMA((len(parts),))],
        input_output_aliases={1 + count: 0} if extra else {},
        compiler_params=pltpu.CompilerParams(vmem_limit_bytes=2**22),
        cost_estimate=pl.CostEstimate(flops=0, bytes_accessed=2 * len(parts) * B * B, transcendentals=0),
        name="place",
    )(info, *held, *extra)


def exchange(pieces, groups):
    return lax.all_to_all(pieces, SLAB, 0, 0, axis_index_groups=groups)


def step(grad_partial, owner_table, left_factor, right_factor, left_precond, right_precond):
    core = lax.axis_index("core")
    quarter = 2 * ((lax.axis_index("y") + core) % 2) + (lax.axis_index("x") + core) % 2
    here = jnp.stack([core, lax.axis_index("zl"), quarter]).astype(jnp.int32)
    info = jnp.concatenate([here, owner_table[0]])

    def fetch(other):
        return call(
            functools.partial(fetch_kernel, other),
            (NZ, B, B),
            (info,),
            (grad_partial[0],),
            scratch=[pltpu.SemaphoreType.DMA((NZ,))],
            cost=2**21,
            space=HBM,
        )

    give = fetch(True)
    got = lax.ppermute(give, "core", SWAP)
    keep = fetch(False)
    pieces = call(pair_kernel, (NEAR, AWAY, NZ, ROWS, B), (info,), (keep, got), cost=2**22)
    in_quad = exchange(pieces.reshape(NEAR, AWAY * NZ, ROWS, B), QUADS)
    part = call(sum_kernel, (AWAY * NZ, ROWS, B), (), (in_quad,), cost=2**21)
    strips = call(spread_kernel, (NEAR * AWAY, ROWS, B), (), (exchange(part, AWAY_Z),), cost=2**20)
    owned = lax.all_to_all(strips, ("y", "x"), 0, 0).reshape(B, B)

    held = [
        pltpu.with_memory_space_constraint(a, VMEM) for a in (left_precond[0, 0], owned, right_precond[0, 0])
    ]
    strip = (B // NEAR, B)
    scaled, strips = pl.pallas_call(
        direction_kernel,
        out_shape=(
            pltpu.VMEM((NEAR,) + strip, jnp.bfloat16),
            jax.ShapeDtypeStruct((NZ,) + strip, jnp.bfloat16),
        ),
        in_specs=[pl.BlockSpec(memory_space=SMEM)] + [pl.BlockSpec(memory_space=VMEM)] * 3,
        out_specs=(pl.BlockSpec(memory_space=VMEM), pl.BlockSpec(memory_space=pl.ANY)),
        scratch_shapes=[
            pltpu.VMEM((NEAR,) + strip, jnp.float32),
            pltpu.VMEM(strip, jnp.bfloat16),
            pltpu.SemaphoreType.DMA((NZ,)),
        ],
        compiler_params=pltpu.CompilerParams(vmem_limit_bytes=2**22),
        cost_estimate=pl.CostEstimate(flops=4 * B**3, bytes_accessed=2**21, transcendentals=0),
        name="scaled",
    )(info, *held)
    scaled_other = lax.ppermute(scaled, "core", SWAP)
    strips = lax.all_to_all(strips, "zl", 0, 0)
    direction = place(info, [(0, 0, 0), (1, 0, 1)], [scaled, scaled_other])
    foreign = call(foreign_kernel, (NEAR, NZ - 1, B // NEAR, B), (info,), (strips,), cost=2**20)
    foreign = exchange(foreign, QUADS)
    foreign_other = lax.ppermute(foreign, "core", SWAP)
    direction = place(info, [(0, 1, 0), (0, 2, 0)], [foreign], direction)
    direction = place(info, [(0, 1, 1), (0, 2, 1)], [foreign_other], direction).reshape(NZ * NC, B, B)

    outer_rows = lax.dot_general(
        owned, owned, (((1,), (1,)), ((), ())), preferred_element_type=jnp.float32
    )
    new_left = (decay * left_factor[0, 0] + (1.0 - decay) * outer_rows)[None, None]
    outer_cols = lax.dot_general(
        owned, owned, (((0,), (0,)), ((), ())), preferred_element_type=jnp.float32
    )
    new_right = (decay * right_factor[0, 0] + (1.0 - decay) * outer_cols)[None, None]
    return (direction, new_left, new_right)


def solution(mesh):
    fine = Mesh(mesh.devices.reshape(NY, NX, NZ, NC, NT), ("y", "x", "zl", "core", "tensor"))
    owner = ("zl", "core")
    placed = (
        P(("y", "x") + owner, "tensor", None, None),
        P("tensor", None),
        P(owner, "tensor", None, None),
        P(owner, "tensor", None, None),
        P(owner, "tensor", None, None),
        P(owner, "tensor", None, None),
    )
    return jax.shard_map(
        step,
        mesh=fine,
        in_specs=placed,
        out_specs=(
            P("tensor", None, None),
            P(owner, "tensor", None, None),
            P(owner, "tensor", None, None),
        ),
        check_vma=False,
    )
```

```python
import functools

import jax
import jax.numpy as jnp
from jax import lax
from jax.experimental import pallas as pl
from jax.experimental.pallas import tpu as pltpu
from jax.sharding import Mesh, PartitionSpec as P


decay = 0.9
epsilon = 1e-06

NY, NX, NZ, NC, NT = 8, 4, 3, 2, 4
B = 512
ROWS = B // (NX * NY)
NEAR, AWAY = 4, 8
SWAP = [(0, 1), (1, 0)]
SLAB = ("y", "x", "zl", "core")
VMEM = pltpu.MemorySpace.VMEM
HBM = pltpu.MemorySpace.HBM
SMEM = pltpu.MemorySpace.SMEM


def device(core, height, quad, member):
    y = (2 * (quad // 2) + member // 2 + core) % NY
    x = (2 * (quad % 2) + member % 2 + core) % NX
    return ((y * NX + x) * NZ + height) * NC + core


QUADS = [[device(c, z, f, q) for q in range(NEAR)] for c in range(NC) for z in range(NZ) for f in range(AWAY)]
AWAY_Z = [
    [device(c, z, f, q) for z in range(NZ) for f in range(AWAY)] for c in range(NC) for q in range(NEAR)
]


def block_of(info_ref, owner):
    found = jnp.int32(0)
    for k in range(NZ * NC):
        found = jnp.where(info_ref[3 + k] == owner, jnp.int32(k), found)
    return found


def call(kernel, out, scalars, arrays, scratch=(), cost=0, space=VMEM):
    held = [pltpu.with_memory_space_constraint(a, space) for a in arrays]
    return pl.pallas_call(
        kernel,
        out_shape=tuple(pltpu.VMEM(o, jnp.bfloat16) for o in out)
        if isinstance(out[0], tuple)
        else pltpu.VMEM(out, jnp.bfloat16),
        in_specs=[pl.BlockSpec(memory_space=SMEM)] * len(scalars)
        + [pl.BlockSpec(memory_space=space)] * len(arrays),
        out_specs=(pl.BlockSpec(memory_space=VMEM),) * len(out)
        if isinstance(out[0], tuple)
        else pl.BlockSpec(memory_space=VMEM),
        scratch_shapes=list(scratch),
        compiler_params=pltpu.CompilerParams(vmem_limit_bytes=2**22),
        cost_estimate=pl.CostEstimate(flops=0, bytes_accessed=cost, transcendentals=0),
    )(*scalars, *held)


def fetch_kernel(other, info_ref, grad_ref, out_ref, sem):
    core = 1 - info_ref[0] if other else info_ref[0]
    copies = [
        pltpu.make_async_copy(grad_ref.at[block_of(info_ref, 2 * z + core)], out_ref.at[z], sem.at[z])
        for z in range(NZ)
    ]
    for copy in copies:
        copy.start()
    for copy in copies:
        copy.wait()


def pair_kernel(info_ref, keep_ref, got_ref, out_ref):
    core = info_ref[0]
    for y in range(NY):
        for x in range(NX):
            up, right = lax.rem(y + NY - core, jnp.int32(NY)), lax.rem(x + NX - core, jnp.int32(NX))
            member = 2 * lax.rem(up, jnp.int32(2)) + lax.rem(right, jnp.int32(2))
            quad = 2 * (up >> 1) + (right >> 1)
            rows = pl.ds((x * NY + y) * ROWS, ROWS)
            for z in range(NZ):
                total = keep_ref[z, rows].astype(jnp.float32) + got_ref[z, rows].astype(jnp.float32)
                out_ref[member, z, quad] = total.astype(out_ref.dtype)


def sum_kernel(terms_ref, out_ref):
    count, pieces = terms_ref.shape[0], terms_ref.shape[1]

    def step(i, carry):
        total = terms_ref[0, i].astype(jnp.float32)
        for t in range(1, count):
            total = total + terms_ref[t, i].astype(jnp.float32)
        out_ref[i] = total.astype(out_ref.dtype)
        return carry

    lax.fori_loop(0, pieces, step, 0, unroll=2)


def spread_kernel(terms_ref, out_ref):
    total = terms_ref[0].astype(jnp.float32)
    for t in range(1, terms_ref.shape[0]):
        total = total + terms_ref[t].astype(jnp.float32)
    strip = total.astype(out_ref.dtype)
    for i in range(out_ref.shape[0]):
        out_ref[i] = strip


def foreign_kernel(info_ref, strips_ref, out_ref):
    for d in range(1, NZ):
        strip = strips_ref[lax.rem(info_ref[1] + NZ - d, jnp.int32(NZ))]
        for i in range(out_ref.shape[0]):
            out_ref[i, d - 1] = strip


def direction_kernel(info_ref, left_ref, owned_ref, right_ref, out_ref, strips_ref, full_ref, strip_ref, sem):
    step = B // NEAR
    square = jnp.zeros((8, 128), jnp.float32)
    for i in range(NEAR):
        rows = pl.ds(i * step, step)
        half = jnp.dot(left_ref[rows], owned_ref[...], preferred_element_type=jnp.float32)
        full = jnp.dot(half.astype(jnp.bfloat16), right_ref[...], preferred_element_type=jnp.float32)
        full_ref[i] = full
        square = square + jnp.sum((full * full).reshape(step // 8, 8, B // 128, 128), axis=(0, 2))
    scale = lax.rsqrt(jnp.sum(square) * (1.0 / (B * B)) + epsilon)
    strip_ref[...] = (full_ref[info_ref[2]] * scale).astype(strip_ref.dtype)
    copies = [pltpu.make_async_copy(strip_ref, strips_ref.at[z], sem.at[z]) for z in range(NZ)]
    for copy in copies:
        copy.start()
    for i in range(NEAR):
        out_ref[i] = (full_ref[i] * scale).astype(out_ref.dtype)
    for copy in copies:
        copy.wait()


def place_kernel(parts, info_ref, *refs):
    out_ref, sem = refs[-2], refs[-1]
    copies = []
    for n, (i, d, s) in enumerate(parts):
        core = info_ref[0] if s == 0 else 1 - info_ref[0]
        z = lax.rem(info_ref[1] + NZ - d, jnp.int32(NZ))
        block = refs[i] if d == 0 else refs[i].at[:, d - 1]
        to = out_ref.at[block_of(info_ref, 2 * z + core)]
        copies.append(pltpu.make_async_copy(block, to, sem.at[n]))
    for copy in copies:
        copy.start()
    for copy in copies:
        copy.wait()


def place(info, parts, arrays, into=None):
    count = len(arrays)
    extra = [] if into is None else [into]
    held = [pltpu.with_memory_space_constraint(a, VMEM) for a in arrays]
    return pl.pallas_call(
        functools.partial(place_kernel, parts),
        out_shape=jax.ShapeDtypeStruct((NZ * NC, NEAR, B // NEAR, B), jnp.bfloat16),
        in_specs=[pl.BlockSpec(memory_space=SMEM)]
        + [pl.BlockSpec(memory_space=VMEM)] * count
        + [pl.BlockSpec(memory_space=pl.ANY)] * len(extra),
        out_specs=pl.BlockSpec(memory_space=pl.ANY),
        scratch_shapes=[pltpu.SemaphoreType.DMA((len(parts),))],
        input_output_aliases={1 + count: 0} if extra else {},
        compiler_params=pltpu.CompilerParams(vmem_limit_bytes=2**22),
        cost_estimate=pl.CostEstimate(flops=0, bytes_accessed=2 * len(parts) * B * B, transcendentals=0),
        name="place",
    )(info, *held, *extra)


def exchange(pieces, groups):
    return lax.all_to_all(pieces, SLAB, 0, 0, axis_index_groups=groups)


def step(grad_partial, owner_table, left_factor, right_factor, left_precond, right_precond):
    core = lax.axis_index("core")
    quarter = 2 * ((lax.axis_index("y") + core) % 2) + (lax.axis_index("x") + core) % 2
    here = jnp.stack([core, lax.axis_index("zl"), quarter]).astype(jnp.int32)
    info = jnp.concatenate([here, owner_table[0]])

    def fetch(other):
        return call(
            functools.partial(fetch_kernel, other),
            (NZ, B, B),
            (info,),
            (grad_partial[0],),
            scratch=[pltpu.SemaphoreType.DMA((NZ,))],
            cost=2**21,
            space=HBM,
        )

    give = fetch(True)
    got = lax.ppermute(give, "core", SWAP)
    keep = fetch(False)
    pieces = call(pair_kernel, (NEAR, NZ, AWAY, ROWS, B), (info,), (keep, got), cost=2**22)
    in_quad = exchange(pieces.reshape(NEAR, AWAY * NZ, ROWS, B), QUADS)
    part = call(sum_kernel, (AWAY * NZ, ROWS, B), (), (in_quad,), cost=2**21)
    strips = call(spread_kernel, (NEAR * AWAY, ROWS, B), (), (exchange(part, AWAY_Z),), cost=2**20)
    owned = lax.all_to_all(strips, ("x", "y"), 0, 0).reshape(B, B)

    held = [
        pltpu.with_memory_space_constraint(a, VMEM) for a in (left_precond[0, 0], owned, right_precond[0, 0])
    ]
    strip = (B // NEAR, B)
    scaled, strips = pl.pallas_call(
        direction_kernel,
        out_shape=(
            pltpu.VMEM((NEAR,) + strip, jnp.bfloat16),
            jax.ShapeDtypeStruct((NZ,) + strip, jnp.bfloat16),
        ),
        in_specs=[pl.BlockSpec(memory_space=SMEM)] + [pl.BlockSpec(memory_space=VMEM)] * 3,
        out_specs=(pl.BlockSpec(memory_space=VMEM), pl.BlockSpec(memory_space=pl.ANY)),
        scratch_shapes=[
            pltpu.VMEM((NEAR,) + strip, jnp.float32),
            pltpu.VMEM(strip, jnp.bfloat16),
            pltpu.SemaphoreType.DMA((NZ,)),
        ],
        compiler_params=pltpu.CompilerParams(vmem_limit_bytes=2**22),
        cost_estimate=pl.CostEstimate(flops=4 * B**3, bytes_accessed=2**21, transcendentals=0),
        name="scaled",
    )(info, *held)
    scaled_other = lax.ppermute(scaled, "core", SWAP)
    strips = lax.all_to_all(strips, "zl", 0, 0)
    direction = place(info, [(0, 0, 0), (1, 0, 1)], [scaled, scaled_other])
    foreign = call(foreign_kernel, (NEAR, NZ - 1, B // NEAR, B), (info,), (strips,), cost=2**20)
    foreign = exchange(foreign, QUADS)
    foreign_other = lax.ppermute(foreign, "core", SWAP)
    direction = place(info, [(0, 1, 0), (0, 2, 0)], [foreign], direction)
    direction = place(info, [(0, 1, 1), (0, 2, 1)], [foreign_other], direction).reshape(NZ * NC, B, B)

    outer_rows = lax.dot_general(
        owned, owned, (((1,), (1,)), ((), ())), preferred_element_type=jnp.float32
    )
    new_left = (decay * left_factor[0, 0] + (1.0 - decay) * outer_rows)[None, None]
    outer_cols = lax.dot_general(
        owned, owned, (((0,), (0,)), ((), ())), preferred_element_type=jnp.float32
    )
    new_right = (decay * right_factor[0, 0] + (1.0 - decay) * outer_cols)[None, None]
    return (direction, new_left, new_right)


def solution(mesh):
    fine = Mesh(mesh.devices.reshape(NY, NX, NZ, NC, NT), ("y", "x", "zl", "core", "tensor"))
    owner = ("zl", "core")
    placed = (
        P(("y", "x") + owner, "tensor", None, None),
        P("tensor", None),
        P(owner, "tensor", None, None),
        P(owner, "tensor", None, None),
        P(owner, "tensor", None, None),
        P(owner, "tensor", None, None),
    )
    return jax.shard_map(
        step,
        mesh=fine,
        in_specs=placed,
        out_specs=(
            P("tensor", None, None),
            P(owner, "tensor", None, None),
            P(owner, "tensor", None, None),
        ),
        check_vma=False,
    )
```
